32 devices in a mesh: row: 8 (over z, x), col: 4 (over y, core).
Axes of the slice: x: 2, y: 2, z: 4, core: 2. Of those that a mesh axis runs over, the one named last changes fastest.
Arguments:
- matrix: float32 [8192, 4096], P('row', 'col'), may hold values from -80 to 80, as said below
Outputs:
- q_panels: float32 [8192, 512], P('row')
- coeff_rows: float32 [512, 4096], P(None, 'col')
- remainder: float32 [8192, 4096], P('row', 'col')
The draws below stay inside these ranges and needn't reach their ends.
Inputs may be any that keep to these rules, and one draw needn't show every extreme that they name: `matrix`: the first 512 columns have full column rank; the other columns are well conditioned against them.
All inputs are finite; a program needn't handle non-finite values.
Results may differ from the reference program's by a relative error of at most 0.0003.
Values sent between devices are 32-bit elements; how exact they have to be, the bound alone decides.
No kernel may reach another device: no remote copies, remote signals or barrier semaphores. Data moves between devices by JAX's collectives and lax.ppermute only.
A program may use at most 64 MiB of HBM per device.

```python
import jax
import jax.numpy as jnp
from jax import lax

PW = 256
CB = 512
ROWS = 8192
COLS = 4096


def draw_matrix(key, part):
    subkeys = jax.random.split(jax.random.fold_in(key, 11), 5)
    position = jnp.arange(ROWS, dtype=jnp.float32) / ROWS
    rising = jnp.exp(0.5 * jnp.log(3.0) * position)
    roughness = jnp.exp(jax.random.uniform(subkeys[0], (ROWS,), minval=-1.15, maxval=1.15))
    row_scale = (rising * roughness)[:, None]
    col_scale = jnp.exp(jax.random.uniform(subkeys[1], (CB,), minval=-1.15, maxval=1.15))[None, :]
    entries = jax.random.truncated_normal(subkeys[2], -4.0, 4.0, (ROWS, CB))
    panel_cols = entries * col_scale * row_scale
    mixing = jax.random.normal(subkeys[3], (CB, COLS - CB)) / jnp.sqrt(float(CB))
    noise_part = jax.random.truncated_normal(subkeys[4], -4.0, 4.0, (ROWS, COLS - CB)) * row_scale
    trailing = jnp.dot(panel_cols, mixing, precision=lax.Precision.HIGHEST) + noise_part
    whole = jnp.concatenate([panel_cols, trailing], axis=1)
    return jnp.clip(whole, -80.0, 80.0).astype(jnp.float32)


def setup_inputs(seed: int = 0) -> dict:
    key_list = jax.random.split(jax.random.key(seed), 2)
    return {
        "matrix": draw_matrix(jax.random.fold_in(key_list[1], 71), 0),
    }


def inverse_factor(gram_matrix):
    factor_low = jnp.linalg.cholesky(gram_matrix)
    identity = jnp.eye(gram_matrix.shape[0], dtype=gram_matrix.dtype)
    return jax.scipy.linalg.solve_triangular(factor_low, identity, lower=True)

def reference(matrix):
    row_count = matrix.shape[0]
    remainder = matrix
    bases = []
    coeffs = []
    for panel_index in range(2):
        panel_cols = remainder[:, panel_index * PW:(panel_index + 1) * PW]
        gram_matrix = jnp.dot(panel_cols.T, panel_cols, precision=lax.Precision.HIGHEST) / row_count
        inverse = inverse_factor(gram_matrix)
        basis = jnp.dot(panel_cols, inverse.T, precision=lax.Precision.HIGHEST)
        coeff_part = jnp.dot(basis.T, remainder, precision=lax.Precision.HIGHEST) / row_count
        remainder = remainder - jnp.dot(basis, coeff_part, precision=lax.Precision.HIGHEST)
        bases.append(basis)
        coeffs.append(coeff_part)
    return (jnp.concatenate(bases, axis=1), jnp.concatenate(coeffs, axis=0), remainder)
```

```python
import functools

import jax
import jax.numpy as jnp
from jax import lax
from jax.experimental import pallas as pl
from jax.experimental.pallas import tpu as pltpu
from jax.sharding import PartitionSpec as P

PW = 256
SUB = 8
NB = 128
AXES = ("row", "col")
HIGHEST = lax.Precision.HIGHEST


def dot(left, right, dim_left, dim_right, precision=HIGHEST):
    return lax.dot_general(
        left,
        right,
        (((dim_left,), (dim_right,)), ((), ())),
        precision=precision,
        preferred_element_type=jnp.float32,
    )


def eliminate_slab(rows, first):
    sub = lax.broadcasted_iota(jnp.int32, (SUB, NB), 0)
    cols = [
        jnp.broadcast_to(rows[:, first + k : first + k + 1], (SUB, NB)) for k in range(SUB)
    ]
    left, right = rows[:, :NB], rows[:, NB:]
    for k in range(SUB):
        root = lax.rsqrt(jnp.broadcast_to(cols[k][k : k + 1, :], (SUB, NB)))
        below = jnp.where(sub > k, cols[k] * root, 0.0)
        pivot_left = jnp.broadcast_to(left[k : k + 1, :], (SUB, NB)) * root
        pivot_right = jnp.broadcast_to(right[k : k + 1, :], (SUB, NB)) * root
        left = jnp.where(sub == k, pivot_left, left - below * pivot_left)
        right = jnp.where(sub == k, pivot_right, right - below * pivot_right)
        for j in range(k + 1, SUB):
            cols[j] = cols[j] - below * (
                jnp.broadcast_to(cols[j][k : k + 1, :], (SUB, NB)) * root
            )
    return jnp.concatenate([left, right], axis=1)


def eliminate_block(ref):
    for lo in range(0, NB, SUB):
        rows = eliminate_slab(ref[lo : lo + SUB, :], lo)
        ref[lo : lo + SUB, :] = rows
        if lo + SUB < NB:
            update = dot(rows[:, :NB], rows, 0, 0)
            ref[lo + SUB :, :] = ref[lo + SUB :, :] - update[lo + SUB :, :]


def inverse_kernel(scale, gram_ref, out_ref, s_ref, w_ref, t_ref):
    n = s_ref.shape[0]
    s_ref[:PW, :] = gram_ref[:, : 2 * PW] * scale
    s_ref[PW:, PW:] = gram_ref[:, 2 * PW :] * scale
    row = lax.broadcasted_iota(jnp.int32, (NB, NB), 0)
    col = lax.broadcasted_iota(jnp.int32, (NB, NB), 1)
    eye = jnp.where(row == col, 1.0, 0.0).astype(jnp.float32)
    w_ref[...] = jnp.zeros_like(w_ref)
    for lo in range(0, n, NB):
        hi = lo + NB
        t_ref[:, :NB] = s_ref[lo:hi, lo:hi]
        t_ref[:, NB:] = eye
        eliminate_block(t_ref)
        w = t_ref[:, NB:]
        if lo:
            w_ref[lo:hi, :lo] = dot(w, w_ref[lo:hi, :lo], 1, 0)
        w_ref[lo:hi, lo:hi] = w
        if hi < n:
            u = dot(w, s_ref[lo:hi, hi:], 1, 0)
            s_ref[hi:, hi:] = s_ref[hi:, hi:] - dot(u, u, 0, 0)
            w_ref[hi:, :hi] = w_ref[hi:, :hi] - dot(u, w_ref[lo:hi, :hi], 0, 0)
    out_ref[:, :PW] = w_ref[:PW, :PW]
    out_ref[:, PW:] = w_ref[PW:, :]


def inverse_factor(gram, scale):
    return pl.pallas_call(
        functools.partial(inverse_kernel, scale),
        out_shape=jax.ShapeDtypeStruct((PW, 3 * PW), jnp.float32),
        in_specs=[pl.BlockSpec(memory_space=pltpu.VMEM)],
        out_specs=pl.BlockSpec(memory_space=pltpu.VMEM),
        scratch_shapes=[
            pltpu.VMEM((2 * PW, 2 * PW), jnp.float32),
            pltpu.VMEM((2 * PW, 2 * PW), jnp.float32),
            pltpu.VMEM((NB, 2 * NB), jnp.float32),
        ],
        name="inverse_factor",
    )(gram)


def broadcast_col(values):
    count = lax.axis_size("col")
    mine = lax.axis_index("col")
    step = count // 2
    while step:
        pairs = [(i, i + step) for i in range(0, count, 2 * step)]
        moved = lax.ppermute(values, "col", pairs)
        values = jnp.where(mine % (2 * step) == step, moved, values)
        step //= 2
    return values


def sum_row(values, cols):
    rows, count = lax.axis_size("row"), lax.axis_size("col")
    bits = list(range(rows.bit_length() - 1))
    swapped = bits[1::-1] + bits[2:]
    orders = [swapped if c % 2 else bits for c in range(count)]
    odd = lax.axis_index("col") % 2
    index = lax.axis_index("row")

    def exchange(piece, step):
        pairs = [
            (r * count + c, (r ^ (1 << orders[c][step])) * count + c)
            for r in range(rows)
            for c in cols
        ]
        return lax.ppermute(piece, AXES, pairs)

    def bit_of(step):
        return jnp.where(odd == 1, index >> swapped[step], index >> bits[step]) & 1

    halved = []
    for step in bits:
        height = values.shape[0] // 2
        if step == bits[-1] or height < SUB:
            values = values + exchange(values, step)
            continue
        bit = bit_of(step)
        kept = lax.dynamic_slice_in_dim(values, bit * height, height, 0)
        sent = lax.dynamic_slice_in_dim(values, (1 - bit) * height, height, 0)
        values = kept + exchange(sent, step)
        halved.append(step)
    for step in reversed(halved):
        other = exchange(values, step)
        first = bit_of(step) == 0
        values = jnp.concatenate(
            [jnp.where(first, values, other), jnp.where(first, other, values)], axis=0
        )
    return values


def on_device(matrix):
    rows = lax.axis_size("row")
    scale = 1.0 / (matrix.shape[0] * rows)
    every = range(lax.axis_size("col"))
    root = lax.axis_index("col") == 0

    own = [matrix[:, :PW], matrix[:, PW : 2 * PW]]
    panels = [broadcast_col(p) for p in own]
    gram = jnp.concatenate(
        [dot(own[0], matrix[:, : 2 * PW], 0, 0), dot(own[1], own[1], 0, 0)], axis=1
    )
    gram = sum_row(gram, [0])
    inverse = lax.cond(
        root, lambda g: inverse_factor(g, scale), lambda g: jnp.zeros_like(g), gram
    )
    inverse = broadcast_col(inverse)
    w00, w10, w11 = (inverse[:, i * PW : (i + 1) * PW] for i in range(3))

    cross = [sum_row(dot(p, matrix, 0, 0), every) for p in panels]
    first = dot(w00, cross[0] * scale, 1, 0)
    second = dot(w10, cross[0] * scale, 1, 0) + dot(w11, cross[1] * scale, 1, 0)
    basis_first = dot(panels[0], w00, 1, 1)
    basis_second = dot(panels[0], w10, 1, 1) + dot(panels[1], w11, 1, 1)
    remainder = matrix - dot(basis_first, first, 1, 0) - dot(basis_second, second, 1, 0)
    return (
        jnp.concatenate([basis_first, basis_second], axis=1),
        jnp.concatenate([first, second], axis=0),
        remainder,
    )


def solution(mesh):
    return jax.shard_map(
        on_device,
        mesh=mesh,
        in_specs=(P("row", "col"),),
        out_specs=(P("row", None), P(None, "col"), P("row", "col")),
        check_vma=False,
    )
```
